32 devices in a mesh: row: 8 (over z, core), col: 4 (over y, x).
Axes of the slice: x: 2, y: 2, z: 4, core: 2. Of those that a mesh axis runs over, the one named last changes fastest.
Arguments:
- samples: bfloat16 [1024, 1024], P('row'), may hold values from -6 to 6
- frequencies: bfloat16 [1024, 16384], P(None, ('row', 'col')), may hold values from -0.375 to 0.375
- phases: bfloat16 [16384], P(('row', 'col')), may hold values from 0 to 6.28125
Outputs:
- gram_matrix: float32 [16384, 16384], P('row', 'col')
The draws below stay inside these ranges and needn't reach their ends.
All inputs are finite; a program needn't handle non-finite values.
Results may differ from the reference program's by a relative error of at most 0.0014.
Values may be sent and summed in bfloat16 or wider, within the bound.
No kernel may reach another device: no remote copies, remote signals or barrier semaphores. Data moves between devices by JAX's collectives and lax.ppermute only.
A program may use at most 128 MiB of HBM per device.

```python
import jax
import jax.numpy as jnp

F = 16384
DIN = 1024
S = 1024
N_ROW = 8
N_COL = 4


def levels(key, dims, cuts, smallest, largest):
    def one(dim, shards_of):
        heights = jax.random.uniform(jax.random.fold_in(jax.random.fold_in(key, 6), dim), (shards_of,), jnp.float32, smallest / len(cuts), largest / len(cuts))
        return jnp.repeat(jnp.exp(heights), dims[dim] // shards_of).reshape((-1,) + (1,) * (len(dims) - dim - 1))

    loudness = one(*cuts[0])
    for cut in cuts[1:]:
        loudness = loudness * one(*cut)
    return loudness


def centred(key, shape, scale, most, shards=(), kind=jnp.bfloat16):
    array = scale * jax.random.normal(key, shape, jnp.float32)
    if shards:
        array = array * levels(key, shape, shards, -0.22, 0.18)
    return jnp.clip(array, -most, most).astype(kind)


def setup_inputs(seed: int = 0) -> dict:
    key_of = jax.random.split(jax.random.key(seed), 4)
    samples = centred(key_of[0], (S, DIN), 1.0, 6.0, ((0, 8),))
    frequencies = centred(key_of[1], (DIN, F), (DIN // 4) ** -0.5, 0.375, ((1, 32),))
    phases = jnp.clip(6.28125 * jax.random.uniform(key_of[2], (F,), jnp.float32) ** levels(key_of[2], (F,), ((0, 32),), -0.2, 0.2), 0.0, 6.28125).astype(jnp.bfloat16)
    return dict(samples=samples, frequencies=frequencies, phases=phases)


def reference(samples, frequencies, phases):
    projected = jnp.dot(samples, frequencies, preferred_element_type=jnp.float32) + phases.astype(jnp.float32)
    features = jnp.cos(projected).astype(jnp.bfloat16)
    sample_count = features.shape[0]
    reordered = features.reshape(sample_count, N_ROW, N_COL, F // (N_ROW * N_COL))
    reordered = reordered.transpose(0, 2, 1, 3).reshape(sample_count, F)
    gram_matrix = jnp.dot(features.T, reordered, preferred_element_type=jnp.float32)
    return gram_matrix * (2.0 / sample_count)
```

```python
import functools

import jax
import jax.numpy as jnp
from jax import lax
from jax.experimental import pallas as pl
from jax.experimental.pallas import tpu as pltpu
from jax.sharding import PartitionSpec as P

ANY = pl.BlockSpec(memory_space=pl.ANY)

COS_TERMS = (
    1.0,
    -0.5,
    0.0416666641831398,
    -0.0013888862449675798,
    2.4800550818326883e-05,
    -2.753474177552562e-07,
    2.0603099226690347e-09,
    -9.72095320905808e-12,
)


def cosine(angle):
    turns = (angle * 0.15915494309189535 + 12582912.0) - 12582912.0
    rest = (angle - turns * 6.28125) - turns * 0.0019353071795864769
    square = rest * rest
    total = jnp.full_like(square, COS_TERMS[-1])
    for term in COS_TERMS[-2::-1]:
        total = total * square + term
    return total


def own_features_kernel(place, near, far, freq, phase, feats, feats_t, ordered, sems, *, q, lanes, sides, blocks):
    step = pl.program_id(0)
    z, core, j = place[0], place[1], place[2]
    rows = ordered.shape[0] // blocks

    @pl.when(step == 0)
    def _():
        for far_side, source in enumerate((near, far)):
            for dj in range(sides):
                for dz in range(lanes):
                    target = ((core ^ far_side) * sides + (j ^ dj)) * lanes + (z ^ dz)
                    pltpu.make_async_copy(
                        source.at[pl.ds((dj * lanes + dz) * q, q)],
                        ordered.at[pl.ds(target * q, q)],
                        sems.at[target * q // rows],
                    ).start()

    block = ordered.at[pl.ds(step * rows, rows)]
    pltpu.make_async_copy(near.at[pl.ds(0, rows)], block, sems.at[step]).wait()
    projected = jnp.dot(block[...], freq[...], preferred_element_type=jnp.float32)
    values = cosine(projected + phase[...].astype(jnp.float32)).astype(jnp.bfloat16)
    feats[...] = values
    feats_t[...] = values.T


def own_features(place, near, far, freq, phase, lanes, sides, blocks=4):
    half, depth = near.shape
    n = freq.shape[1]
    total = 2 * half
    rows = total // blocks
    return pl.pallas_call(
        functools.partial(
            own_features_kernel, q=half // (lanes * sides), lanes=lanes, sides=sides, blocks=blocks
        ),
        grid_spec=pltpu.PrefetchScalarGridSpec(
            num_scalar_prefetch=1,
            grid=(blocks,),
            in_specs=[
                ANY,
                ANY,
                pl.BlockSpec((depth, n), lambda b, place: (0, 0)),
                pl.BlockSpec((1, n), lambda b, place: (0, 0)),
            ],
            out_specs=[
                pl.BlockSpec((rows, n), lambda b, place: (b, 0)),
                pl.BlockSpec((n, rows), lambda b, place: (0, b)),
            ],
            scratch_shapes=[
                pltpu.VMEM((total, depth), near.dtype),
                pltpu.SemaphoreType.DMA((blocks,)),
            ],
        ),
        out_shape=[
            jax.ShapeDtypeStruct((total, n), jnp.bfloat16),
            jax.ShapeDtypeStruct((n, total), jnp.bfloat16),
        ],
        cost_estimate=pl.CostEstimate(
            flops=2 * total * depth * n, bytes_accessed=2 * total * depth, transcendentals=total * n
        ),
        name="own_features",
    )(place, near, far, freq, phase)


def gram_kernel(place, *refs, n_rows, n_cols, scale, chained):
    lefts, rights = refs[:n_rows], refs[n_rows : n_rows + n_cols]
    out = refs[n_rows + n_cols + (1 if chained else 0)]
    left_buf, right_buf, tile_buf, left_sem, right_sem, out_sem = refs[-6:]
    n, m = tile_buf.shape[1:]

    def left_copy(r):
        return pltpu.make_async_copy(lefts[r], left_buf.at[r], left_sem.at[r])

    def right_copy(c):
        return pltpu.make_async_copy(rights[c], right_buf.at[c], right_sem.at[c])

    def out_copy(t):
        c, r, slot = t // n_rows, t % n_rows, t % 2
        target = out.at[
            pl.ds(pl.multiple_of(place[r] * n, n), n),
            pl.ds(pl.multiple_of(place[n_rows + c] * m, m), m),
        ]
        return pltpu.make_async_copy(tile_buf.at[slot], target, out_sem.at[slot])

    right_copy(0).start()
    for r in range(n_rows):
        left_copy(r).start()
    for c in range(1, n_cols):
        right_copy(c).start()

    def tile(t, carry):
        c, r = t // n_rows, t % n_rows
        for k in range(n_cols):
            @pl.when(t == k * n_rows)
            def _():
                right_copy(k).wait()
        for k in range(n_rows):
            @pl.when(t == k)
            def _():
                left_copy(k).wait()

        @pl.when(t >= 2)
        def _():
            out_copy(t - 2).wait()

        tile_buf[t % 2] = scale * jnp.dot(left_buf[r], right_buf[c], preferred_element_type=jnp.float32)
        out_copy(t).start()
        return carry

    tiles = n_rows * n_cols
    lax.fori_loop(0, tiles, tile, 0)
    for t in range(max(tiles - 2, 0), tiles):
        out_copy(t).wait()


def gram(acc, lefts, rights, left_at, right_at, shape, scale):
    n, total = lefts[0].shape
    m = rights[0].shape[1]
    n_rows, n_cols = len(lefts), len(rights)
    place = jnp.stack([jnp.asarray(v, jnp.int32) for v in (*left_at, *right_at)])
    chained = acc is not None
    operands = (place, *lefts, *rights) + ((acc,) if chained else ())
    return pl.pallas_call(
        functools.partial(gram_kernel, n_rows=n_rows, n_cols=n_cols, scale=scale, chained=chained),
        grid_spec=pltpu.PrefetchScalarGridSpec(
            num_scalar_prefetch=1,
            grid=(),
            in_specs=[ANY] * (len(operands) - 1),
            out_specs=ANY,
            scratch_shapes=[
                pltpu.VMEM((n_rows, n, total), lefts[0].dtype),
                pltpu.VMEM((n_cols, total, m), rights[0].dtype),
                pltpu.VMEM((2, n, m), jnp.float32),
                pltpu.SemaphoreType.DMA((n_rows,)),
                pltpu.SemaphoreType.DMA((n_cols,)),
                pltpu.SemaphoreType.DMA((2,)),
            ],
        ),
        out_shape=jax.ShapeDtypeStruct(shape, jnp.float32),
        input_output_aliases={len(operands) - 1: 0} if chained else {},
        cost_estimate=pl.CostEstimate(
            flops=2 * n_rows * n_cols * n * total * m,
            bytes_accessed=2 * total * (n * n_rows + m * n_cols) + 4 * n * n_rows * m * n_cols,
            transcendentals=0,
        ),
        name="gram",
    )(*operands)


def swap(x, axis, bits):
    return lax.ppermute(x, axis, [(i, i ^ bits) for i in range(lax.axis_size(axis))])


def line(x, pairs):
    return lax.ppermute(x, "row", [(2 * a + k, 2 * b + k) for a, b in pairs for k in range(2)])


def by_links(samples, frequencies, phases):
    n_row, n_col = lax.axis_size("row"), lax.axis_size("col")
    chips = n_row // 2
    i, j = lax.axis_index("row"), lax.axis_index("col")
    z, core = i // 2, i % 2
    n = frequencies.shape[1]
    total = samples.shape[0] * n_row
    scale = 2.0 / total
    shape = (n * n_col, n * n_row)
    q = samples.shape[0] // n_col

    part = lax.dynamic_slice_in_dim(samples, j * q, q)
    column = jnp.concatenate([part] + [swap(part, "row", 2 * d) for d in range(1, chips)])
    near = jnp.concatenate([column] + [swap(column, "col", d) for d in range(1, n_col)])
    far = swap(near, "row", 1)

    place = jnp.stack([z, core, j]).astype(jnp.int32)
    own, own_t = own_features(place, near, far, frequencies, phases[None, :], chips, n_col)

    outer, inner = [(0, 1), (1, 0), (2, 3), (3, 2)], [(1, 2), (2, 1)]
    outward = [(1, 0), (2, 3)]
    end = (z == 0) | (z == 3)
    a1 = line(own, outer)
    b1 = line(own, inner)
    x1 = swap(own_t, "col", 1)
    y1 = swap(own_t, "col", 2)
    own_c = swap(own, "row", 1)
    a2 = line(b1, outward)
    b2 = line(a1, inner)
    a1_c = swap(a1, "row", 1)
    half = n // 2
    d_low = swap(x1[:half], "col", 2)
    d_high = swap(y1[half:], "col", 1)
    diagonal = jnp.concatenate([d_low, d_high])
    a3 = line(b2, outward)
    v2 = jnp.where(end, a2, b1)
    v2_c = swap(v2, "row", 1)
    v3 = jnp.where(end, a3, b2)
    v3_c = swap(v3, "row", 1)

    z1 = z ^ 1
    z2 = jnp.where(z < 2, 2, 1)
    z2 = jnp.where(end, z2, 3 - z)
    z3 = 3 - z
    z3 = jnp.where(end, z3, jnp.where(z == 1, 3, 0))
    at = lambda zz: [2 * zz + core, 2 * zz + (core ^ 1)]
    acc = gram(None, [own_t], [own, own_c, a1, a1_c], [j], at(z) + at(z1), shape, scale)
    acc = gram(acc, [x1, y1], [own, own_c, a1, a1_c], [j ^ 1, j ^ 2], at(z) + at(z1), shape, scale)
    acc = gram(acc, [own_t, x1, y1], [v2, v2_c], [j, j ^ 1, j ^ 2], at(z2), shape, scale)
    acc = gram(acc, [diagonal], [own, own_c, a1, a1_c, v2, v2_c], [j ^ 3], at(z) + at(z1) + at(z2), shape, scale)
    acc = gram(acc, [own_t, x1, y1, diagonal], [v3, v3_c], [j, j ^ 1, j ^ 2, j ^ 3], at(z3), shape, scale)
    return acc


def by_gathers(samples, frequencies, phases):
    everyone = lax.all_gather(samples, "row", axis=0, tiled=True)
    projected = jnp.dot(everyone, frequencies, preferred_element_type=jnp.float32)
    feats = cosine(projected + phases.astype(jnp.float32)).astype(jnp.bfloat16)
    left = lax.all_gather(feats, "col", axis=1, tiled=True)
    right = lax.all_gather(feats, "row", axis=1, tiled=True)
    tile = lax.dot_general(left, right, (((0,), (0,)), ((), ())), preferred_element_type=jnp.float32)
    return tile * (2.0 / everyone.shape[0])


def solution(mesh):
    in_specs = (P("row", None), P(None, ("row", "col")), P(("row", "col")))
    out_specs = P("row", "col")
    short = mesh.shape["row"] == 8 and mesh.shape["col"] == 4
    body = by_links if short else by_gathers
    return jax.shard_map(body, mesh=mesh, in_specs=in_specs, out_specs=out_specs, check_vma=False)
```

```python
import functools

import jax
import jax.numpy as jnp
from jax import lax
from jax.experimental import pallas as pl
from jax.experimental.pallas import tpu as pltpu
from jax.sharding import PartitionSpec as P


ANY = pl.BlockSpec(memory_space=pl.ANY)
VMEM = pl.BlockSpec(memory_space=pltpu.VMEM)
SMEM = pl.BlockSpec(memory_space=pltpu.SMEM)

PAD = 8

COS_TERMS = (
    1.0,
    -0.49999988079071045,
    0.04166648909449577,
    -0.0013887799577787519,
    2.4769791707512923e-05,
    -2.707812996050052e-07,
    1.7241773564435903e-09,
)


def cosine(angle):
    turns = (angle * 0.15915494309189535 + 12582912.0) - 12582912.0
    rest = (angle - turns * 6.28125) - turns * 0.0019353071795864769
    square = rest * rest
    total = square * COS_TERMS[-1] + COS_TERMS[-2]
    for term in COS_TERMS[-3::-1]:
        total = total * square + term
    return total


def features_of(block, freq, phase):
    projected = jnp.dot(block, freq, preferred_element_type=jnp.float32)
    return cosine(projected + phase).astype(jnp.bfloat16)


def phase_of(part, n):
    return part[part.shape[0] - PAD :, :n][0:1].astype(jnp.float32)


Z, CORE, J, END, HELD = 0, 1, 2, 3, 4


def own_features_kernel(place, *refs, lanes, sides, rows):
    pieces, (part, freq, feats, feats_t, low_t, high_t, ordered) = refs[:-7], refs[-7:]
    q = pieces[0].shape[0] // lanes
    for k, piece in enumerate(pieces):
        side = (place[CORE] ^ (k // sides)) * sides + (place[J] ^ (k % sides))
        for dz in range(lanes):
            at = pl.multiple_of((side * lanes + (place[Z] ^ dz)) * q, q)
            ordered[pl.ds(at, q), :] = piece[pl.ds(dz * q, q), :]
    n = feats.shape[1]
    phase = phase_of(part, n)
    for b in range(feats.shape[0] // rows):
        at = pl.ds(b * rows, rows)
        values = features_of(ordered[at, :], freq[...], phase)
        feats[at, :] = values
        turned = values.T
        feats_t[:, at] = turned
        low_t[:, at] = turned[: n // 2]
        high_t[:, at] = turned[n // 2 :]


def own_features(place, pieces, part, freq, lanes, sides, rows=256):
    depth, n = freq.shape
    total = sum(piece.shape[0] for piece in pieces)
    shapes = [(total, n), (n, total), (n // 2, total), (n // 2, total), (total, depth)]
    return pl.pallas_call(
        functools.partial(own_features_kernel, lanes=lanes, sides=sides, rows=rows),
        in_specs=[SMEM] + [VMEM] * (len(pieces) + 2),
        out_specs=[VMEM] * 5,
        out_shape=[jax.ShapeDtypeStruct(shape, jnp.bfloat16) for shape in shapes],
        compiler_params=pltpu.CompilerParams(vmem_limit_bytes=16 << 20),
        cost_estimate=pl.CostEstimate(
            flops=2 * total * depth * n, bytes_accessed=4 * total * depth, transcendentals=0
        ),
        name="own_features",
    )(place, *pieces, part, freq)


def features_kernel(place, samples, *refs, inputs, first, width, rows, joined):
    refs = list(refs)
    count = inputs
    sources, parts = refs[:count], refs[count : 2 * count]
    rest = refs[2 * count :]
    n = sources[0].shape[1]
    freq, phase = None, None
    if count == 1:
        freq, phase = sources[0], phase_of(parts[0], n)
    else:
        freq = rest.pop()
        for k, source in enumerate(sources):
            @pl.when(place[END] == k)
            def _():
                freq[...] = source[...]

        phase = jnp.where(place[END] == 0, phase_of(parts[0], n), phase_of(parts[1], n))
    feats = rest[-1]
    columns = slice(first, first + width)
    if joined:
        before, feats, whole = rest
        whole[:, :first] = before[...]
    for b in range(samples.shape[0] // rows):
        at = pl.ds(b * rows, rows)
        values = features_of(samples[at, :], freq[:, columns], phase[:, columns])
        feats[at, :] = values
        if joined:
            whole[at, columns] = values


def features(place, samples, sources, parts, first=0, width=None, before=None, rows=256):
    total, depth = samples.shape
    n = sources[0].shape[1]
    width = width or n
    joined = before is not None
    shapes = [(total, width)] + ([(total, n)] if joined else [])
    out = pl.pallas_call(
        functools.partial(features_kernel, inputs=len(sources), first=first, width=width, rows=rows, joined=joined),
        in_specs=[SMEM] + [VMEM] * (1 + 2 * len(sources) + joined),
        out_specs=[VMEM] * len(shapes),
        scratch_shapes=[pltpu.VMEM(sources[0].shape, sources[0].dtype)] if len(sources) > 1 else [],
        out_shape=[jax.ShapeDtypeStruct(shape, jnp.bfloat16) for shape in shapes],
        compiler_params=pltpu.CompilerParams(vmem_limit_bytes=12 << 20),
        cost_estimate=pl.CostEstimate(
            flops=2 * total * depth * width, bytes_accessed=2 * total * depth, transcendentals=0
        ),
        name="features",
    )(place, samples, *sources, *parts, *([before] if joined else []))
    return out if joined else out[0]


def gram_kernel(place, *refs, lefts, blocks, tiles, scale, chained, n):
    refs = list(refs)
    left_refs = [[refs.pop(0) for _ in range(parts)] for _, parts in lefts]
    right_refs = [[[refs.pop(0) for _ in range(piece[-1])] for piece in block] for block in blocks]
    if chained:
        refs.pop(0)
    out = refs.pop(0)
    sems, tile_buf = refs.pop(), refs.pop()
    slots = tile_buf.shape[0]

    left_bufs = []
    for parts in left_refs:
        if len(parts) == 1:
            left_bufs.append(parts[0])
            continue
        kept, at = refs.pop(0), 0
        for part in parts:
            kept[pl.ds(at, part.shape[0]), :] = part[...]
            at += part.shape[0]
        left_bufs.append(kept)
    right_bufs = []
    for pieces in right_refs:
        if len(pieces) == 1 and len(pieces[0]) == 1:
            right_bufs.append(pieces[0][0])
            continue
        held, at = refs.pop(0), 0
        for sources in pieces:
            width = sources[0].shape[1]
            for k, source in enumerate(sources):
                if len(sources) == 1:
                    held[:, at : at + width] = source[...]
                else:
                    @pl.when(place[END] == k)
                    def _():
                        held[:, at : at + width] = source[...]
            at += width
        right_bufs.append(held)

    def out_copies(t):
        left, block = tiles[t]
        copies = []
        for r, which in enumerate(lefts[left][0]):
            row = which ^ place[J]
            at = 0
            for chip, core, first, width, _ in blocks[block]:
                column = (place[HELD + chip] * 2 + (place[CORE] ^ core)) * n + first
                copies.append(
                    pltpu.make_async_copy(
                        tile_buf.at[t % slots, pl.ds(r * n, n), pl.ds(at, width)],
                        out.at[pl.ds(pl.multiple_of(row * n, n), n), pl.ds(pl.multiple_of(column, width), width)],
                        sems.at[t % slots, len(copies)],
                    )
                )
                at += width
        return copies

    for t, (left, block) in enumerate(tiles):
        if t >= slots:
            for copy in out_copies(t - slots):
                copy.wait()
        product = jnp.dot(left_bufs[left][...], right_bufs[block][...], preferred_element_type=jnp.float32)
        tile_buf[t % slots, pl.ds(0, product.shape[0]), pl.ds(0, product.shape[1])] = product * scale
        for copy in out_copies(t):
            copy.start()
    for t in range(max(len(tiles) - slots, 0), len(tiles)):
        for copy in out_copies(t):
            copy.wait()


def gram(acc, place, lefts, blocks, tiles, shape, scale, slots=3):
    total = lefts[0][1][0].shape[1]
    described = [[(chip, core, first, a[0].shape[1], len(a)) for chip, core, first, a in block] for block in blocks]
    heights = [sum(part.shape[0] for part in parts) for _, parts in lefts]
    widths = [sum(piece[3] for piece in block) for block in described]
    chained = acc is not None
    operands = [part for _, parts in lefts for part in parts]
    operands += [source for block in blocks for piece in block for source in piece[3]]
    joined = [height for height, (_, parts) in zip(heights, lefts) if len(parts) > 1]
    held = [width for width, block in zip(widths, described) if len(block) > 1 or block[0][-1] > 1]
    copies = max(len(lefts[left][0]) * len(described[block]) for left, block in tiles)
    tall, wide = max(heights[left] for left, _ in tiles), max(widths[block] for _, block in tiles)
    products = sum(heights[left] * widths[block] for left, block in tiles)
    out = pl.pallas_call(
        functools.partial(
            gram_kernel,
            lefts=[(which, len(parts)) for which, parts in lefts],
            blocks=described,
            tiles=tiles,
            scale=scale,
            chained=chained,
            n=heights[0] // len(lefts[0][0]),
        ),
        in_specs=[SMEM] + [VMEM] * len(operands) + ([ANY] if chained else []),
        out_specs=[ANY] + [VMEM] * len(joined),
        scratch_shapes=[pltpu.VMEM((total, width), jnp.bfloat16) for width in held]
        + [pltpu.VMEM((slots, tall, wide), jnp.float32), pltpu.SemaphoreType.DMA((slots, copies))],
        out_shape=[jax.ShapeDtypeStruct(shape, jnp.float32)]
        + [jax.ShapeDtypeStruct((height, total), jnp.bfloat16) for height in joined],
        input_output_aliases={len(operands) + 1: 0} if chained else {},
        compiler_params=pltpu.CompilerParams(vmem_limit_bytes=16 << 20),
        cost_estimate=pl.CostEstimate(flops=2 * total * products, bytes_accessed=4 * products, transcendentals=0),
        name="gram",
    )(place, *operands, *([acc] if chained else []))
    return out if joined else out[0]


def swap(x, axis, bits):
    return lax.ppermute(x, axis, [(i, i ^ bits) for i in range(lax.axis_size(axis))])


def line(x, pairs):
    return lax.ppermute(x, "row", [(2 * a + k, 2 * b + k) for a, b in pairs for k in range(2)])


def by_links(samples, frequencies, phases):
    n_row, n_col = lax.axis_size("row"), lax.axis_size("col")
    chips = n_row // 2
    i, j = lax.axis_index("row"), lax.axis_index("col")
    z, core = i // 2, i % 2
    depth, n = frequencies.shape
    half = n // 2
    scale = 2.0 / (samples.shape[0] * n_row)
    shape = (n * n_col, n * n_row)
    q = samples.shape[0] // n_col
    outer, inner, outward = [(0, 1), (1, 0), (2, 3), (3, 2)], [(1, 2), (2, 1)], [(1, 0), (2, 3)]

    end = (z == 0) | (z == 3)
    held2 = jnp.where(end, jnp.where(z < 2, 2, 1), 3 - z)
    held3 = jnp.where(end, 3 - z, jnp.where(z == 1, 3, 0))
    place = jnp.stack([z, core, j, end.astype(jnp.int32), z, z ^ 1, held2, held3]).astype(jnp.int32)

    padded = jnp.pad(jnp.broadcast_to(phases[None, :], (PAD, n)), ((0, 0), (0, depth - n)))
    part = jnp.concatenate([lax.dynamic_slice_in_dim(samples, j * q, q), padded])
    parts = [part] + [swap(part, "row", 2 * d) for d in range(1, chips)]
    column = jnp.concatenate([p[:q] for p in parts])
    near = [column] + [swap(column, "col", d) for d in range(1, n_col)]
    far = [swap(piece, "row", 1) for piece in near]

    b1 = line(frequencies, inner)
    a1 = line(frequencies, outer)
    a2 = line(b1, outward)

    own, own_t, low, high, everyone = own_features(place, near + far, part, frequencies, chips, n_col)
    x_low = swap(low, "col", 1)
    y_high = swap(high, "col", 2)
    x_high = swap(high, "col", 1)
    y_low = swap(low, "col", 2)
    own_c = swap(own, "row", 1)
    f1a = features(place, everyone, [a1], [parts[1]], 0, half)
    b2a = line(f1a, inner)
    f1b, f1 = features(place, everyone, [a1], [parts[1]], half, half, f1a)
    b2b = line(f1b, inner)
    f1_c = swap(f1, "row", 1)
    d_low = swap(x_low, "col", 2)
    d_high = swap(y_high, "col", 1)
    f2 = features(place, everyone, [b1, a2], [parts[3], parts[2]])
    f2_c = swap(f2, "row", 1)
    a3a = line(b2a, outward)
    a3b = line(b2b, outward)
    b2a_c = swap(b2a, "row", 1)
    b2b_c = swap(b2b, "row", 1)
    a3a_c = swap(a3a, "row", 1)
    a3b_c = swap(a3b, "row", 1)

    def pair(chip, mine, others):
        return [[(chip, 0, 0, [mine])], [(chip, 1, 0, [others])]]

    def grid(rows, columns):
        return [(r, c) for c in range(columns) for r in range(rows)]

    first = pair(0, own, own_c) + pair(1, f1, f1_c)
    acc = gram(None, place, [((0,), [own_t])], first, grid(1, 4), shape, scale)
    acc, across = gram(acc, place, [((1, 2), [x_low, x_high, y_low, y_high])], first, grid(1, 4), shape, scale)
    known = [((0,), [own_t]), ((1, 2), [across])]
    acc = gram(acc, place, known, pair(2, f2, f2_c), grid(2, 2), shape, scale)
    blocks = first + pair(2, f2, f2_c)
    acc, diagonal = gram(acc, place, [((3,), [d_low, d_high])], blocks, grid(1, 6), shape, scale)
    known = [((1, 2), [across]), ((0,), [own_t]), ((3,), [diagonal])]
    blocks = [[(3, 0, 0, [b2a, a3a]), (3, 1, 0, [b2a_c, a3a_c])]]
    acc = gram(acc, place, known, blocks, grid(3, 1), shape, scale)
    blocks = [[(3, 0, half, [b2b, a3b]), (3, 1, half, [b2b_c, a3b_c])]]
    acc = gram(acc, place, known, blocks, grid(3, 1), shape, scale)
    return acc


def by_gathers(samples, frequencies, phases):
    everyone = lax.all_gather(samples, "row", axis=0, tiled=True)
    projected = jnp.dot(everyone, frequencies, preferred_element_type=jnp.float32)
    feats = cosine(projected + phases.astype(jnp.float32)).astype(jnp.bfloat16)
    left = lax.all_gather(feats, "col", axis=1, tiled=True)
    right = lax.all_gather(feats, "row", axis=1, tiled=True)
    tile = lax.dot_general(left, right, (((0,), (0,)), ((), ())), preferred_element_type=jnp.float32)
    return tile * (2.0 / everyone.shape[0])


def solution(mesh):
    specs = dict(
        mesh=mesh,
        in_specs=(P("row", None), P(None, ("row", "col")), P(("row", "col"))),
        out_specs=P("row", "col"),
        check_vma=False,
    )
    if mesh.shape["row"] != 8 or mesh.shape["col"] != 4:
        return jax.shard_map(by_gathers, **specs)

    return jax.shard_map(by_links, **specs)
```

```python
import functools

import jax
import jax.numpy as jnp
from jax import lax
from jax.experimental import pallas as pl
from jax.experimental.pallas import tpu as pltpu
from jax.sharding import PartitionSpec as P


ANY = pl.BlockSpec(memory_space=pl.ANY)
HBM = pl.BlockSpec(memory_space=pltpu.HBM)
VMEM = pl.BlockSpec(memory_space=pltpu.VMEM)

LANES = 128

COS_TERMS = (
    1.0,
    -0.49999988079071045,
    0.04166648909449577,
    -0.0013887799577787519,
    2.4769791707512923e-05,
    -2.707812996050052e-07,
    1.7241773564435903e-09,
)


def cosine(angle):
    turns = (angle * 0.15915494309189535 + 12582912.0) - 12582912.0
    rest = (angle - turns * 6.28125) - turns * 0.0019353071795864769
    square = rest * rest
    total = square * COS_TERMS[-1] + COS_TERMS[-2]
    for term in COS_TERMS[-3::-1]:
        total = total * square + term
    return total


def features_of(block, freq, phase):
    projected = jnp.dot(block, freq, preferred_element_type=jnp.float32)
    return cosine(projected + phase).astype(jnp.bfloat16)


def phase_of(part, depth, n):
    held = part[:, depth:].astype(jnp.float32)
    return jnp.concatenate([held[r : r + 1] for r in range(n // LANES)], axis=1)


def part_kernel(samples, phases, part, given, sems):
    q = part.shape[0]
    depth, n = samples.shape[1], phases.shape[0]
    at = pl.ds(pl.multiple_of(lax.axis_index("col") * q, q), q)
    copy = pltpu.make_async_copy(samples.at[at, :], part.at[:, pl.ds(0, depth)], sems.at[0])
    copy.start()
    phases_copy = pltpu.make_async_copy(phases, given, sems.at[1])
    phases_copy.start()
    phases_copy.wait()
    flat = given[...].astype(jnp.float32).reshape(1, n)
    rows = [flat[:, r * LANES : (r + 1) * LANES] for r in range(n // LANES)]
    rows.append(jnp.zeros((q - len(rows), LANES), jnp.float32))
    part[:, depth:] = jnp.concatenate(rows, axis=0).astype(part.dtype)
    copy.wait()


def part_of(samples, phases, q):
    return pl.pallas_call(
        part_kernel,
        in_specs=[HBM, HBM],
        out_specs=VMEM,
        out_shape=jax.ShapeDtypeStruct((q, samples.shape[1] + LANES), samples.dtype),
        scratch_shapes=[pltpu.VMEM(phases.shape, phases.dtype), pltpu.SemaphoreType.DMA((2,))],
        compiler_params=pltpu.CompilerParams(vmem_limit_bytes=4 << 20),
        name="part",
    )(samples, phases)


def near_kernel(array, copy, sem):
    move = pltpu.make_async_copy(array, copy, sem)
    move.start()
    move.wait()


def bring_near(array):
    return pl.pallas_call(
        near_kernel,
        in_specs=[ANY],
        out_specs=VMEM,
        out_shape=jax.ShapeDtypeStruct(array.shape, array.dtype),
        scratch_shapes=[pltpu.SemaphoreType.DMA],
        compiler_params=pltpu.CompilerParams(vmem_limit_bytes=4 << 20),
        cost_estimate=pl.CostEstimate(flops=0, bytes_accessed=4 * array.size, transcendentals=0),
        name="bring_near",
    )(array)


class Place:
    def __init__(self):
        row = lax.axis_index("row")
        self.z, self.core, self.j = lax.shift_right_logical(row, 1), row & 1, lax.axis_index("col")
        self.end = ((self.z ^ lax.shift_right_logical(self.z, 1)) & 1) ^ 1
        crossed, opposite = self.z ^ 3, self.z ^ 2
        self.held = (self.z, self.z ^ 1, jnp.where(self.end == 1, opposite, crossed), jnp.where(self.end == 1, crossed, opposite))


def own_features_kernel(*refs, lanes, sides, rows):
    place = Place()
    pieces, (part, freq, feats, feats_t, low_t, high_t, ordered) = refs[:-7], refs[-7:]
    q = pieces[0].shape[0] // lanes
    for k, piece in enumerate(pieces):
        side = (place.core ^ (k // sides)) * sides + (place.j ^ (k % sides))
        for dz in range(lanes):
            at = pl.multiple_of((side * lanes + (place.z ^ dz)) * q, q)
            ordered[pl.ds(at, q), :] = piece[pl.ds(dz * q, q), :]
    n = feats.shape[1]
    phase = phase_of(part, freq.shape[0], n)
    for b in range(feats.shape[0] // rows):
        at = pl.ds(b * rows, rows)
        values = features_of(ordered[at, :], freq[...], phase)
        feats[at, :] = values
        turned = values.T
        feats_t[:, at] = turned
        low_t[:, at] = turned[: n // 2]
        high_t[:, at] = turned[n // 2 :]


def own_features(pieces, part, freq, lanes, sides, rows=256):
    depth, n = freq.shape
    total = sum(piece.shape[0] for piece in pieces)
    shapes = [(total, n), (n, total), (n // 2, total), (n // 2, total), (total, depth)]
    return pl.pallas_call(
        functools.partial(own_features_kernel, lanes=lanes, sides=sides, rows=rows),
        in_specs=[VMEM] * (len(pieces) + 2),
        out_specs=[VMEM] * 5,
        out_shape=[jax.ShapeDtypeStruct(shape, jnp.bfloat16) for shape in shapes],
        compiler_params=pltpu.CompilerParams(vmem_limit_bytes=16 << 20),
        cost_estimate=pl.CostEstimate(
            flops=2 * total * depth * n, bytes_accessed=4 * total * depth, transcendentals=0
        ),
        name="own_features",
    )(*pieces, part, freq)


def features_kernel(samples, *refs, inputs, first, width, rows, joined):
    place = Place()
    refs = list(refs)
    count = len(inputs)
    sources = [[refs.pop(0) for _ in range(pieces)] for pieces in inputs]
    parts, rest = refs[:count], refs[count:]
    n = sources[0][0].shape[1]
    freq, phase = None, None
    if count == 1:
        freq, phase = sources[0][0], phase_of(parts[0], samples.shape[1], n)
    else:
        freq = rest.pop()
        for k, source in enumerate(sources):
            @pl.when(place.end == k)
            def _():
                at = 0
                for piece in source:
                    freq[pl.ds(at, piece.shape[0]), :] = piece[...]
                    at += piece.shape[0]

        phase = jnp.where(place.end == 0, phase_of(parts[0], samples.shape[1], n), phase_of(parts[1], samples.shape[1], n))
    feats = rest[-1]
    columns = slice(first, first + width)
    if joined:
        before, feats, whole = rest
        whole[:, :first] = before[...]
    for b in range(samples.shape[0] // rows):
        at = pl.ds(b * rows, rows)
        values = features_of(samples[at, :], freq[:, columns], phase[:, columns])
        feats[at, :] = values
        if joined:
            whole[at, columns] = values


def features(samples, sources, parts, first=0, width=None, before=None, rows=256):
    total, depth = samples.shape
    n = sources[0][0].shape[1]
    width = width or n
    pieces = [piece for source in sources for piece in source]
    joined = before is not None
    shapes = [(total, width)] + ([(total, n)] if joined else [])
    out = pl.pallas_call(
        functools.partial(features_kernel, inputs=[len(source) for source in sources], first=first, width=width, rows=rows, joined=joined),
        in_specs=[VMEM] * (1 + len(pieces) + len(sources) + joined),
        out_specs=[VMEM] * len(shapes),
        scratch_shapes=[pltpu.VMEM((depth, n), pieces[0].dtype)] if len(sources) > 1 else [],
        out_shape=[jax.ShapeDtypeStruct(shape, jnp.bfloat16) for shape in shapes],
        compiler_params=pltpu.CompilerParams(vmem_limit_bytes=12 << 20),
        cost_estimate=pl.CostEstimate(
            flops=2 * total * depth * width, bytes_accessed=2 * total * depth, transcendentals=0
        ),
        name="features",
    )(samples, *pieces, *parts, *([before] if joined else []))
    return out if joined else out[0]


def gram_kernel(*refs, lefts, blocks, tiles, scale, chained, n):
    place = Place()
    refs = list(refs)
    left_refs = [[refs.pop(0) for _ in range(parts)] for _, parts in lefts]
    right_refs = [[[refs.pop(0) for _ in range(piece[-1])] for piece in block] for block in blocks]
    if chained:
        refs.pop(0)
    out = refs.pop(0)
    sems, tile_buf = refs.pop(), refs.pop()
    slots = tile_buf.shape[0]

    left_bufs = []
    for parts in left_refs:
        if len(parts) == 1:
            left_bufs.append(parts[0])
            continue
        kept, at = refs.pop(0), 0
        for part in parts:
            kept[pl.ds(at, part.shape[0]), :] = part[...]
            at += part.shape[0]
        left_bufs.append(kept)
    right_bufs = []
    for pieces in right_refs:
        if len(pieces) == 1 and len(pieces[0]) == 1:
            right_bufs.append(pieces[0][0])
            continue
        held, at = refs.pop(0), 0
        for sources in pieces:
            width = sources[0].shape[1]
            for k, source in enumerate(sources):
                if len(sources) == 1:
                    held[:, at : at + width] = source[...]
                else:
                    @pl.when(place.end == k)
                    def _():
                        held[:, at : at + width] = source[...]
            at += width
        right_bufs.append(held)

    def out_copies(t):
        left, block = tiles[t]
        copies = []
        for r, which in enumerate(lefts[left][0]):
            row = which ^ place.j
            at = 0
            for chip, core, first, width, _ in blocks[block]:
                column = (place.held[chip] * 2 + (place.core ^ core)) * n + first
                copies.append(
                    pltpu.make_async_copy(
                        tile_buf.at[t % slots, pl.ds(r * n, n), pl.ds(at, width)],
                        out.at[pl.ds(pl.multiple_of(row * n, n), n), pl.ds(pl.multiple_of(column, width), width)],
                        sems.at[t % slots, len(copies)],
                    )
                )
                at += width
        return copies

    for t, (left, block) in enumerate(tiles):
        if t >= slots:
            for copy in out_copies(t - slots):
                copy.wait()
        product = jnp.dot(left_bufs[left][...], right_bufs[block][...], preferred_element_type=jnp.float32)
        tile_buf[t % slots, pl.ds(0, product.shape[0]), pl.ds(0, product.shape[1])] = product * scale
        for copy in out_copies(t):
            copy.start()
    for t in range(max(len(tiles) - slots, 0), len(tiles)):
        for copy in out_copies(t):
            copy.wait()


def gram(acc, lefts, blocks, tiles, shape, scale, slots=3):
    total = lefts[0][1][0].shape[1]
    described = [[(chip, core, first, a[0].shape[1], len(a)) for chip, core, first, a in block] for block in blocks]
    heights = [sum(part.shape[0] for part in parts) for _, parts in lefts]
    widths = [sum(piece[3] for piece in block) for block in described]
    chained = acc is not None
    operands = [part for _, parts in lefts for part in parts]
    operands += [source for block in blocks for piece in block for source in piece[3]]
    joined = [height for height, (_, parts) in zip(heights, lefts) if len(parts) > 1]
    held = [width for width, block in zip(widths, described) if len(block) > 1 or block[0][-1] > 1]
    copies = max(len(lefts[left][0]) * len(described[block]) for left, block in tiles)
    tall, wide = max(heights[left] for left, _ in tiles), max(widths[block] for _, block in tiles)
    products = sum(heights[left] * widths[block] for left, block in tiles)
    out = pl.pallas_call(
        functools.partial(
            gram_kernel,
            lefts=[(which, len(parts)) for which, parts in lefts],
            blocks=described,
            tiles=tiles,
            scale=scale,
            chained=chained,
            n=heights[0] // len(lefts[0][0]),
        ),
        in_specs=[VMEM] * len(operands) + ([ANY] if chained else []),
        out_specs=[ANY] + [VMEM] * len(joined),
        scratch_shapes=[pltpu.VMEM((total, width), jnp.bfloat16) for width in held]
        + [pltpu.VMEM((slots, tall, wide), jnp.float32), pltpu.SemaphoreType.DMA((slots, copies))],
        out_shape=[jax.ShapeDtypeStruct(shape, jnp.float32)]
        + [jax.ShapeDtypeStruct((height, total), jnp.bfloat16) for height in joined],
        input_output_aliases={len(operands): 0} if chained else {},
        compiler_params=pltpu.CompilerParams(vmem_limit_bytes=16 << 20),
        cost_estimate=pl.CostEstimate(flops=2 * total * products, bytes_accessed=4 * products, transcendentals=0),
        name="gram",
    )(*operands, *([acc] if chained else []))
    return out if joined else out[0]


def swap(x, axis, bits):
    return lax.ppermute(x, axis, [(i, i ^ bits) for i in range(lax.axis_size(axis))])


def line(x, pairs):
    return lax.ppermute(x, "row", [(2 * a + k, 2 * b + k) for a, b in pairs for k in range(2)])


def by_links(samples, frequencies, phases):
    n_row, n_col = lax.axis_size("row"), lax.axis_size("col")
    chips = n_row // 2
    depth, n = frequencies.shape
    half = n // 2
    scale = 2.0 / (samples.shape[0] * n_row)
    shape = (n * n_col, n * n_row)
    q = samples.shape[0] // n_col
    outer, inner, outward = [(0, 1), (1, 0), (2, 3), (3, 2)], [(1, 2), (2, 1)], [(1, 0), (2, 3)]

    part = part_of(samples, phases, q)
    parts = [part] + [swap(part, "row", 2 * d) for d in range(1, chips)]
    column = jnp.concatenate([p[:, :depth] for p in parts])
    near = [column] + [swap(column, "col", d) for d in range(1, n_col)]
    far = [swap(piece, "row", 1) for piece in near]

    a1 = line(frequencies, outer)
    b1a = line(frequencies[: depth // 2], inner)
    _, later = lax.optimization_barrier((column, frequencies))
    b1b = line(later[depth // 2 :], inner)
    a2a = line(b1a, outward)
    a2b = line(b1b, outward)

    freq = bring_near(frequencies)
    own, own_t, low, high, everyone = own_features(near + far, part, freq, chips, n_col)
    x_low = swap(low, "col", 1)
    y_high = swap(high, "col", 2)
    x_high = swap(high, "col", 1)
    y_low = swap(low, "col", 2)
    own_c = swap(own, "row", 1)
    f1a = features(everyone, [[a1]], [parts[1]], 0, half)
    b2a = line(f1a, inner)
    f1b, f1 = features(everyone, [[a1]], [parts[1]], half, half, f1a)
    b2b = line(f1b, inner)
    f1_c = swap(f1, "row", 1)
    d_low = swap(x_low, "col", 2)
    d_high = swap(y_high, "col", 1)
    f2 = features(everyone, [[b1a, b1b], [a2a, a2b]], [parts[3], parts[2]])
    f2_c = swap(f2, "row", 1)
    a3a = line(b2a, outward)
    a3b = line(b2b, outward)
    b2a_c = swap(b2a, "row", 1)
    b2b_c = swap(b2b, "row", 1)
    a3a_c = swap(a3a, "row", 1)
    a3b_c = swap(a3b, "row", 1)

    def pair(chip, mine, others):
        return [[(chip, 0, 0, [mine])], [(chip, 1, 0, [others])]]

    def grid(rows, columns):
        return [(r, c) for c in range(columns) for r in range(rows)]

    first = pair(0, own, own_c) + pair(1, f1, f1_c)
    acc = gram(None, [((0,), [own_t])], first, grid(1, 4), shape, scale)
    acc, across = gram(acc, [((1, 2), [x_low, x_high, y_low, y_high])], first, grid(1, 4), shape, scale)
    known = [((1, 2), [across]), ((0,), [own_t])]
    second = pair(2, f2, f2_c)
    acc = gram(acc, known, second, grid(2, 2), shape, scale)
    acc, diagonal = gram(acc, [((3,), [d_low, d_high])], first + second, grid(1, 6), shape, scale)
    known.append(((3,), [diagonal]))
    blocks = [[(3, 0, 0, [b2a, a3a]), (3, 1, 0, [b2a_c, a3a_c])]]
    acc = gram(acc, known, blocks, grid(3, 1), shape, scale)
    blocks = [[(3, 0, half, [b2b, a3b]), (3, 1, half, [b2b_c, a3b_c])]]
    acc = gram(acc, known, blocks, grid(3, 1), shape, scale)
    return acc


def by_gathers(samples, frequencies, phases):
    everyone = lax.all_gather(samples, "row", axis=0, tiled=True)
    projected = jnp.dot(everyone, frequencies, preferred_element_type=jnp.float32)
    feats = cosine(projected + phases.astype(jnp.float32)).astype(jnp.bfloat16)
    left = lax.all_gather(feats, "col", axis=1, tiled=True)
    right = lax.all_gather(feats, "row", axis=1, tiled=True)
    tile = lax.dot_general(left, right, (((0,), (0,)), ((), ())), preferred_element_type=jnp.float32)
    return tile * (2.0 / everyone.shape[0])


def solution(mesh):
    specs = dict(
        mesh=mesh,
        in_specs=(P("row", None), P(None, ("row", "col")), P(("row", "col"))),
        out_specs=P("row", "col"),
        check_vma=False,
    )
    if mesh.shape["row"] != 8 or mesh.shape["col"] != 4:
        return jax.shard_map(by_gathers, **specs)

    return jax.shard_map(by_links, **specs)
```

```python
import functools

import jax
import jax.numpy as jnp
from jax import lax
from jax.experimental import pallas as pl
from jax.experimental.pallas import tpu as pltpu
from jax.sharding import PartitionSpec as P


ANY = pl.BlockSpec(memory_space=pl.ANY)
HBM = pl.BlockSpec(memory_space=pltpu.HBM)
VMEM = pl.BlockSpec(memory_space=pltpu.VMEM)

LANES = 128

COS_TERMS = (
    1.0,
    -0.49999988079071045,
    0.04166648909449577,
    -0.0013887799577787519,
    2.4769791707512923e-05,
    -2.707812996050052e-07,
    1.7241773564435903e-09,
)


def cosine(angle):
    turns = (angle * 0.15915494309189535 + 12582912.0) - 12582912.0
    rest = (angle - turns * 6.28125) - turns * 0.0019353071795864769
    square = rest * rest
    total = square * COS_TERMS[-1] + COS_TERMS[-2]
    for term in COS_TERMS[-3::-1]:
        total = total * square + term
    return total


def features_of(block, freq, phase):
    projected = jnp.dot(block, freq, preferred_element_type=jnp.float32)
    return cosine(projected + phase).astype(jnp.bfloat16)


def phase_of(part, depth, n):
    held = part[:, depth:].astype(jnp.float32)
    return jnp.concatenate([held[r : r + 1] for r in range(n // LANES)], axis=1)


def part_kernel(samples, phases, part, given, sems):
    q = part.shape[0]
    depth, n = samples.shape[1], phases.shape[0]
    at = pl.ds(pl.multiple_of(lax.axis_index("col") * q, q), q)
    copy = pltpu.make_async_copy(samples.at[at, :], part.at[:, pl.ds(0, depth)], sems.at[0])
    copy.start()
    phases_copy = pltpu.make_async_copy(phases, given, sems.at[1])
    phases_copy.start()
    phases_copy.wait()
    flat = given[...].astype(jnp.float32).reshape(1, n)
    rows = [flat[:, r * LANES : (r + 1) * LANES] for r in range(n // LANES)]
    rows.append(jnp.zeros((q - len(rows), LANES), jnp.float32))
    part[:, depth:] = jnp.concatenate(rows, axis=0).astype(part.dtype)
    copy.wait()


def part_of(samples, phases, q):
    return pl.pallas_call(
        part_kernel,
        in_specs=[HBM, HBM],
        out_specs=VMEM,
        out_shape=jax.ShapeDtypeStruct((q, samples.shape[1] + LANES), samples.dtype),
        scratch_shapes=[pltpu.VMEM(phases.shape, phases.dtype), pltpu.SemaphoreType.DMA((2,))],
        compiler_params=pltpu.CompilerParams(vmem_limit_bytes=4 << 20),
        name="part",
    )(pltpu.with_memory_space_constraint(samples, pltpu.HBM), pltpu.with_memory_space_constraint(phases, pltpu.HBM))


def near_kernel(array, copy, sem):
    move = pltpu.make_async_copy(array, copy, sem)
    move.start()
    move.wait()


def bring_near(array):
    return pl.pallas_call(
        near_kernel,
        in_specs=[ANY],
        out_specs=VMEM,
        out_shape=jax.ShapeDtypeStruct(array.shape, array.dtype),
        scratch_shapes=[pltpu.SemaphoreType.DMA],
        compiler_params=pltpu.CompilerParams(vmem_limit_bytes=4 << 20),
        cost_estimate=pl.CostEstimate(flops=0, bytes_accessed=4 * array.size, transcendentals=0),
        name="bring_near",
    )(array)


class Place:
    def __init__(self):
        row = lax.axis_index("row")
        self.z, self.core, self.j = lax.shift_right_logical(row, 1), row & 1, lax.axis_index("col")
        self.end = ((self.z ^ lax.shift_right_logical(self.z, 1)) & 1) ^ 1
        crossed, opposite = self.z ^ 3, self.z ^ 2
        self.held = (self.z, self.z ^ 1, jnp.where(self.end == 1, opposite, crossed), jnp.where(self.end == 1, crossed, opposite))


def own_features_kernel(*refs, lanes, sides, rows):
    place = Place()
    pieces, (part, freq, feats, feats_t, low_t, high_t, ordered) = refs[:-7], refs[-7:]
    q = pieces[0].shape[0] // lanes
    for k, piece in enumerate(pieces):
        side = (place.core ^ (k // sides)) * sides + (place.j ^ (k % sides))
        for dz in range(lanes):
            at = pl.multiple_of((side * lanes + (place.z ^ dz)) * q, q)
            ordered[pl.ds(at, q), :] = piece[pl.ds(dz * q, q), :]
    n = feats.shape[1]
    phase = phase_of(part, freq.shape[0], n)
    for b in range(feats.shape[0] // rows):
        at = pl.ds(b * rows, rows)
        values = features_of(ordered[at, :], freq[...], phase)
        feats[at, :] = values
        turned = values.T
        feats_t[:, at] = turned
        low_t[:, at] = turned[: n // 2]
        high_t[:, at] = turned[n // 2 :]


def own_features(pieces, part, freq, lanes, sides, rows=256):
    depth, n = freq.shape
    total = sum(piece.shape[0] for piece in pieces)
    shapes = [(total, n), (n, total), (n // 2, total), (n // 2, total), (total, depth)]
    return pl.pallas_call(
        functools.partial(own_features_kernel, lanes=lanes, sides=sides, rows=rows),
        in_specs=[VMEM] * (len(pieces) + 2),
        out_specs=[VMEM] * 5,
        out_shape=[jax.ShapeDtypeStruct(shape, jnp.bfloat16) for shape in shapes],
        compiler_params=pltpu.CompilerParams(vmem_limit_bytes=16 << 20),
        cost_estimate=pl.CostEstimate(
            flops=2 * total * depth * n, bytes_accessed=4 * total * depth, transcendentals=0
        ),
        name="own_features",
    )(*pieces, part, freq)


def features_kernel(samples, *refs, n, first, width, sources, befores, tails, rows):
    place = Place()
    refs = list(refs)
    freqs, parts, before, tail = ([refs.pop(0) for _ in range(k)] for k in (sources, sources, befores, tails))
    depth = samples.shape[1]
    columns = slice(first, first + width)
    if sources == 1:
        freq, phase = freqs[0], phase_of(parts[0], depth, n)[:, columns]
        taken = columns if freq.shape[1] == n else slice(0, width)
    else:
        freq, taken = refs.pop(), slice(0, width)
        for k in range(sources):
            @pl.when(place.end == k)
            def _():
                freq[...] = freqs[k][...]

        middle, outer = (phase_of(part, depth, n)[:, columns] for part in parts)
        phase = jnp.where(place.end == 1, outer, middle)
    whole = refs[-1]
    for k in range(befores):
        whole[:, :first] = before[k][...]
    for k in range(tails):
        @pl.when(place.end == k)
        def _():
            whole[:, first + width :] = tail[k][...]

    for b in range(samples.shape[0] // rows):
        at = pl.ds(b * rows, rows)
        values = features_of(samples[at, :], freq[:, taken], phase)
        if not tails:
            refs[0][at, :] = values
        if befores or tails:
            whole[at, columns] = values


def features(samples, sources, parts, n, first, width, before=(), tail=(), rows=256):
    total, depth = samples.shape
    shapes = ([] if tail else [(total, width)]) + ([(total, n)] if before or tail else [])
    out = pl.pallas_call(
        functools.partial(
            features_kernel,
            n=n,
            first=first,
            width=width,
            sources=len(sources),
            befores=len(before),
            tails=len(tail),
            rows=rows,
        ),
        in_specs=[VMEM] * (1 + 2 * len(sources) + len(before) + len(tail)),
        out_specs=[VMEM] * len(shapes),
        scratch_shapes=[pltpu.VMEM((depth, width), sources[0].dtype)] if len(sources) > 1 else [],
        out_shape=[jax.ShapeDtypeStruct(shape, jnp.bfloat16) for shape in shapes],
        compiler_params=pltpu.CompilerParams(vmem_limit_bytes=12 << 20),
        cost_estimate=pl.CostEstimate(
            flops=2 * total * depth * width, bytes_accessed=2 * total * depth, transcendentals=0
        ),
        name="features",
    )(samples, *sources, *parts, *before, *tail)
    return out if len(shapes) > 1 else out[0]


def gram_kernel(*refs, lefts, blocks, tiles, scale, chained, n):
    place = Place()
    refs = list(refs)
    left_refs = [[refs.pop(0) for _ in range(parts)] for _, parts in lefts]
    right_refs = [[[refs.pop(0) for _ in range(piece[-1])] for piece in block] for block in blocks]
    if chained:
        refs.pop(0)
    out = refs.pop(0)
    sems, tile_buf = refs.pop(), refs.pop()
    slots = tile_buf.shape[0]

    left_bufs = []
    for parts in left_refs:
        if len(parts) == 1:
            left_bufs.append(parts[0])
            continue
        kept, at = refs.pop(0), 0
        for part in parts:
            kept[pl.ds(at, part.shape[0]), :] = part[...]
            at += part.shape[0]
        left_bufs.append(kept)
    right_bufs = []
    for pieces in right_refs:
        if len(pieces) == 1 and len(pieces[0]) == 1:
            right_bufs.append(pieces[0][0])
            continue
        held, at = refs.pop(0), 0
        for sources in pieces:
            width = sources[0].shape[1]
            for k, source in enumerate(sources):
                if len(sources) == 1:
                    held[:, at : at + width] = source[...]
                else:
                    @pl.when(place.end == k)
                    def _():
                        held[:, at : at + width] = source[...]
            at += width
        right_bufs.append(held)

    def out_copies(t):
        left, block = tiles[t]
        copies = []
        for r, which in enumerate(lefts[left][0]):
            row = which ^ place.j
            at = 0
            for chip, core, first, width, _ in blocks[block]:
                column = (place.held[chip] * 2 + (place.core ^ core)) * n + first
                copies.append(
                    pltpu.make_async_copy(
                        tile_buf.at[t % slots, pl.ds(r * n, n), pl.ds(at, width)],
                        out.at[pl.ds(pl.multiple_of(row * n, n), n), pl.ds(pl.multiple_of(column, width), width)],
                        sems.at[t % slots, len(copies)],
                    )
                )
                at += width
        return copies

    for t, (left, block) in enumerate(tiles):
        if t >= slots:
            for copy in out_copies(t - slots):
                copy.wait()
        product = jnp.dot(left_bufs[left][...], right_bufs[block][...], preferred_element_type=jnp.float32)
        tile_buf[t % slots, pl.ds(0, product.shape[0]), pl.ds(0, product.shape[1])] = product * scale
        for copy in out_copies(t):
            copy.start()
    for t in range(max(len(tiles) - slots, 0), len(tiles)):
        for copy in out_copies(t):
            copy.wait()


def gram(acc, lefts, blocks, tiles, shape, scale, slots=3):
    total = lefts[0][1][0].shape[1]
    described = [[(chip, core, first, a[0].shape[1], len(a)) for chip, core, first, a in block] for block in blocks]
    heights = [sum(part.shape[0] for part in parts) for _, parts in lefts]
    widths = [sum(piece[3] for piece in block) for block in described]
    chained = acc is not None
    operands = [part for _, parts in lefts for part in parts]
    operands += [source for block in blocks for piece in block for source in piece[3]]
    joined = [height for height, (_, parts) in zip(heights, lefts) if len(parts) > 1]
    held = [width for width, block in zip(widths, described) if len(block) > 1 or block[0][-1] > 1]
    copies = max(len(lefts[left][0]) * len(described[block]) for left, block in tiles)
    tall, wide = max(heights[left] for left, _ in tiles), max(widths[block] for _, block in tiles)
    products = sum(heights[left] * widths[block] for left, block in tiles)
    out = pl.pallas_call(
        functools.partial(
            gram_kernel,
            lefts=[(which, len(parts)) for which, parts in lefts],
            blocks=described,
            tiles=tiles,
            scale=scale,
            chained=chained,
            n=heights[0] // len(lefts[0][0]),
        ),
        in_specs=[VMEM] * len(operands) + ([ANY] if chained else []),
        out_specs=[ANY] + [VMEM] * len(joined),
        scratch_shapes=[pltpu.VMEM((total, width), jnp.bfloat16) for width in held]
        + [pltpu.VMEM((slots, tall, wide), jnp.float32), pltpu.SemaphoreType.DMA((slots, copies))],
        out_shape=[jax.ShapeDtypeStruct(shape, jnp.float32)]
        + [jax.ShapeDtypeStruct((height, total), jnp.bfloat16) for height in joined],
        input_output_aliases={len(operands): 0} if chained else {},
        compiler_params=pltpu.CompilerParams(vmem_limit_bytes=16 << 20),
        cost_estimate=pl.CostEstimate(flops=2 * total * products, bytes_accessed=4 * products, transcendentals=0),
        name="gram",
    )(*operands, *([acc] if chained else []))
    return out if joined else out[0]


def swap(x, axis, bits):
    return lax.ppermute(x, axis, [(i, i ^ bits) for i in range(lax.axis_size(axis))])


def line(x, pairs):
    return lax.ppermute(x, "row", [(2 * a + k, 2 * b + k) for a, b in pairs for k in range(2)])


def by_links(samples, frequencies, phases):
    n_row, n_col = lax.axis_size("row"), lax.axis_size("col")
    chips = n_row // 2
    depth, n = frequencies.shape
    half = n // 2
    scale = 2.0 / (samples.shape[0] * n_row)
    shape = (n * n_col, n * n_row)
    q = samples.shape[0] // n_col
    outer, inner, outward = [(0, 1), (1, 0), (2, 3), (3, 2)], [(1, 2), (2, 1)], [(1, 0), (2, 3)]

    part = part_of(samples, phases, q)
    parts = [part] + [swap(part, "row", 2 * d) for d in range(1, chips)]
    column = jnp.concatenate([p[:, :depth] for p in parts])
    near = [column] + [swap(column, "col", d) for d in range(1, n_col)]
    far = [swap(piece, "row", 1) for piece in near]

    a1 = line(frequencies, outer)
    b1a = line(frequencies[:, :half], inner)
    _, later = lax.optimization_barrier((column, frequencies))
    b1b = line(later[:, half:], inner)
    a2a = line(b1a, outward)

    freq = bring_near(frequencies)
    own, own_t, low, high, everyone = own_features(near + far, part, freq, chips, n_col)
    x_low = swap(low, "col", 1)
    y_high = swap(high, "col", 2)
    x_high = swap(high, "col", 1)
    y_low = swap(low, "col", 2)
    own_c = swap(own, "row", 1)
    f1a = features(everyone, [a1], [parts[1]], n, 0, half)
    b2a = line(f1a, inner)
    f2b = features(everyone, [b1b], [parts[3]], n, half, half)
    a2b = line(f2b, outward)
    f1b, f1 = features(everyone, [a1], [parts[1]], n, half, half, before=[f1a])
    b2b = line(f1b, inner)
    f1_c = swap(f1, "row", 1)
    d_low = swap(x_low, "col", 2)
    d_high = swap(y_high, "col", 1)
    f2 = features(everyone, [b1a, a2a], [parts[3], parts[2]], n, 0, half, tail=[f2b, a2b])
    f2_c = swap(f2, "row", 1)
    a3a = line(b2a, outward)
    a3b = line(b2b, outward)
    b2a_c = swap(b2a, "row", 1)
    b2b_c = swap(b2b, "row", 1)
    a3a_c = swap(a3a, "row", 1)
    a3b_c = swap(a3b, "row", 1)

    def pair(chip, mine, others):
        return [[(chip, 0, 0, [mine])], [(chip, 1, 0, [others])]]

    def grid(rows, columns):
        return [(r, c) for c in range(columns) for r in range(rows)]

    first = pair(0, own, own_c) + pair(1, f1, f1_c)
    acc = gram(None, [((0,), [own_t])], first, grid(1, 4), shape, scale)
    acc, across = gram(acc, [((1, 2), [x_low, x_high, y_low, y_high])], first, grid(1, 4), shape, scale)
    known = [((1, 2), [across]), ((0,), [own_t])]
    second = pair(2, f2, f2_c)
    acc = gram(acc, known, second, grid(2, 2), shape, scale)
    acc, diagonal = gram(acc, [((3,), [d_low, d_high])], first + second, grid(1, 6), shape, scale)
    known.append(((3,), [diagonal]))
    blocks = [[(3, 0, 0, [b2a, a3a]), (3, 1, 0, [b2a_c, a3a_c])]]
    acc = gram(acc, known, blocks, grid(3, 1), shape, scale)
    blocks = [[(3, 0, half, [b2b, a3b]), (3, 1, half, [b2b_c, a3b_c])]]
    acc = gram(acc, known, blocks, grid(3, 1), shape, scale)
    return acc


def by_gathers(samples, frequencies, phases):
    everyone = lax.all_gather(samples, "row", axis=0, tiled=True)
    projected = jnp.dot(everyone, frequencies, preferred_element_type=jnp.float32)
    feats = cosine(projected + phases.astype(jnp.float32)).astype(jnp.bfloat16)
    left = lax.all_gather(feats, "col", axis=1, tiled=True)
    right = lax.all_gather(feats, "row", axis=1, tiled=True)
    tile = lax.dot_general(left, right, (((0,), (0,)), ((), ())), preferred_element_type=jnp.float32)
    return tile * (2.0 / everyone.shape[0])


def solution(mesh):
    specs = dict(
        mesh=mesh,
        in_specs=(P("row", None), P(None, ("row", "col")), P(("row", "col"))),
        out_specs=P("row", "col"),
        check_vma=False,
    )
    if mesh.shape["row"] != 8 or mesh.shape["col"] != 4:
        return jax.shard_map(by_gathers, **specs)

    return jax.shard_map(by_links, **specs)
```
